512 devices in a mesh: seq: 64 (over x, y, core), dp: 8 (over z).
Axes of the slice: x: 4, y: 8, z: 8, core: 2. Of those that a mesh axis runs over, the one named last changes fastest.
Arguments:
- query_proj: bfloat16 [163840, 1024], P(('dp', 'seq')), parts along dimension 0, may hold values from -8 to 8
- key_proj: bfloat16 [163840, 1024], P(('dp', 'seq')), parts along dimension 0, may hold values from -8 to 8
- value_proj: bfloat16 [163840, 1024], P(('dp', 'seq')), parts along dimension 0, may hold values from -6 to 6
- residual_in: bfloat16 [163840, 1024], P(('dp', 'seq')), parts along dimension 0, may hold values from -6 to 6
- utter_lengths: int32 [512], P('dp'), parts along dimension 0, may hold values from 1 to 640, 20480 in all
- depth_kernel: float32 [31, 1024], replicated, may hold values from -1 to 1
- norm_gain: float32 [1024], replicated, may hold values from 0.5 to 1.5
- norm_shift: float32 [1024], replicated, may hold values from -3 to 3
Outputs:
- block_out: bfloat16 [163840, 1024], P(('dp', 'seq')), parts along dimension 0
The draws below stay inside these ranges and needn't reach their ends.
There are 8 independent parts, one for each index of `dp`. The reference program is written for one: setup_inputs(seed, part) draws one part's arguments, and reference() takes and returns one part's arrays. A program takes and returns all parts, laid end to end along the dimension named above; an argument that names none is the same for every part. Nothing has to cross between parts.
Inputs may be any that keep to these rules, and one draw needn't show every extreme that they name: `utter_lengths`: the lengths sum to 20480; the largest is exactly 640.
All inputs are finite; a program needn't handle non-finite values.
Results may differ from the reference program's by a relative error of at most 0.005.
Values may be sent and summed in bfloat16 or wider, within the bound.
A program may use at most 64 MiB of HBM per device.

```python
import math
import jax
import jax.numpy as jnp
import numpy as np
from jax import lax

HD = 64
D = 1024
KERNEL = 31
ROWS = 320
FRAMES = 20480
UTTS = 64
N_SEQ = 64


def shared_pair(key):
    query_base = jnp.clip(jax.random.normal(jax.random.fold_in(key, 11), (FRAMES, D), jnp.float32), -8.0, 8.0)
    key_base = jnp.clip(jax.random.normal(jax.random.fold_in(key, 12), (FRAMES, D), jnp.float32), -8.0, 8.0)
    return (query_base, key_base)


def draw_query_proj(key, part):
    return shared_pair(key)[0].astype(jnp.bfloat16)


def draw_key_proj(key, part):
    return shared_pair(key)[1].astype(jnp.bfloat16)


def block_scale(key, shape, cuts, low, top_value):
    def one(axis_at, shards_of):
        draws = jax.random.uniform(jax.random.fold_in(jax.random.fold_in(key, 6), axis_at), (shards_of,), jnp.float32, low / len(cuts), top_value / len(cuts))
        return jnp.repeat(jnp.exp(draws), shape[axis_at] // shards_of).reshape((-1,) + (1,) * (len(shape) - axis_at - 1))

    gain = one(*cuts[0])
    for cut in cuts[1:]:
        gain = gain * one(*cut)
    return gain


def length_profile(amount, total, most, slope):
    portions = [(1 << 20) // math.isqrt(rank ** slope) + 1 for rank in range(2, amount + 1)]
    rest, given = total - most - (amount - 1), [1] * (amount - 1)
    while rest > 0:
        free = [i for i in range(amount - 1) if given[i] < most]
        pool, remaining = sum([portions[i] for i in free]), rest
        for i in free:
            extra = min(most - given[i], max(1, remaining * portions[i] // pool), rest)
            given[i] = given[i] + extra
            rest = rest - extra
    return np.array([most] + given)


def ragged(rng, amount, total, most, lean):
    if amount == 2:
        one = jax.random.randint(rng, (), max(1, total - most), min(most, total - 1) + 1)
        return jnp.stack([one, total - one])
    tallies = jnp.asarray(length_profile(amount, total, most, lean), jnp.int32)
    twos = (amount - 1) // 2
    donor, receiver = tallies[1:1 + 2 * twos:2], tallies[2:2 + 2 * twos:2]
    room = jnp.minimum(donor - 1, most - receiver)
    passed = jax.random.randint(jax.random.fold_in(rng, 1), (twos,), 0, 1 << 20) % (room + 1)
    tallies = tallies.at[1:1 + 2 * twos:2].set(donor - passed).at[2:2 + 2 * twos:2].set(receiver + passed)
    return tallies[jax.random.permutation(jax.random.fold_in(rng, 2), amount)]


def normal_values(own_key, dims, deviation, bound, shards=(), held_as=jnp.bfloat16):
    drawn = deviation * jax.random.normal(own_key, dims, jnp.float32)
    if shards:
        drawn = drawn * block_scale(own_key, dims, shards, -0.22, 0.18)
    return jnp.clip(drawn, -bound, bound).astype(held_as)


def setup_inputs(seed: int = 0, part: int = 0) -> dict:
    key_of = jax.random.split(jax.random.key(seed), 9)
    part_splits = jax.random.split(jax.random.fold_in(key_of[8], part), 9)
    return {
        "query_proj": draw_query_proj(jax.random.fold_in(jax.random.fold_in(key_of[8], part), 71), part),
        "key_proj": draw_key_proj(jax.random.fold_in(jax.random.fold_in(key_of[8], part), 71), part),
        "value_proj": normal_values(part_splits[2], (FRAMES, D), 1.0, 6.0, ((0, 64),)),
        "residual_in": normal_values(part_splits[3], (FRAMES, D), 1.0, 6.0, ((0, 64),)),
        "utter_lengths": ragged(part_splits[4], UTTS, FRAMES, 2 * ROWS, 1).astype(jnp.int32),
        "depth_kernel": normal_values(key_of[5], (KERNEL, D), KERNEL ** -0.5, 1.0, (), jnp.float32),
        "norm_gain": jnp.clip(1.0 + 0.1 * jax.random.normal(key_of[6], (D,), jnp.float32), 0.5, 1.5),
        "norm_shift": normal_values(key_of[7], (D,), 0.5, 3.0, (), jnp.float32),
    }


def utterance_ids(positions, utt_ends, frames_all):
    counted = lax.optimization_barrier(jnp.sum((utt_ends[None, :] <= positions[:, None]).astype(jnp.int32), axis=1))
    inside = (positions >= 0) & (positions < frames_all)
    return jnp.where(inside, counted, -1).astype(jnp.int32)

def attend(query_rows, query_pos, key_rows, value_rows, key_pos, utt_ends, frames_all):
    query_utt = utterance_ids(query_pos, utt_ends, frames_all)
    key_utt = utterance_ids(key_pos, utt_ends, frames_all)
    same_utt = (query_utt[:, None] == key_utt[None, :])[None]
    score_scale = HD ** (-0.5)
    group_width = 2 * HD
    pieces = []
    for first_col in range(0, query_rows.shape[1], group_width):
        query_group = query_rows[:, first_col:first_col + group_width].reshape(-1, 2, HD).astype(jnp.float32)
        key_group = key_rows[:, first_col:first_col + group_width].reshape(-1, 2, HD).astype(jnp.float32)
        value_group = value_rows[:, first_col:first_col + group_width].reshape(-1, 2, HD).astype(jnp.float32)
        scores = jnp.einsum('qhd,khd->hqk', query_group, key_group) * score_scale
        scores = jnp.where(same_utt, scores, jnp.float32(-1e+30))
        row_max = lax.optimization_barrier(jnp.max(scores, axis=-1, keepdims=True))
        probs = jnp.where(same_utt, jnp.exp(scores - row_max), jnp.float32(0.0))
        denom = lax.optimization_barrier(jnp.sum(probs, axis=-1))
        weights = probs.astype(jnp.bfloat16).astype(jnp.float32)
        context = jnp.einsum('hqk,khd->qhd', weights, value_group) / denom.T[:, :, None]
        pieces.append(context.reshape(context.shape[0], group_width))
    return jnp.concatenate(pieces, axis=1)

def reference(query_proj, key_proj, value_proj, residual_in, utter_lengths, depth_kernel, norm_gain, norm_shift):
    utt_ends = jnp.cumsum(utter_lengths).astype(jnp.int32)
    margin = 2 * ROWS
    key_padded = jnp.pad(key_proj, ((margin, margin), (0, 0)))
    value_padded = jnp.pad(value_proj, ((margin, margin), (0, 0)))

    def one_block(block_index):
        first_row = block_index * ROWS
        query_rows = lax.dynamic_slice_in_dim(query_proj, first_row, ROWS, 0)
        key_rows = lax.dynamic_slice_in_dim(key_padded, first_row, 5 * ROWS, 0)
        value_rows = lax.dynamic_slice_in_dim(value_padded, first_row, 5 * ROWS, 0)
        query_pos = first_row + jnp.arange(ROWS, dtype=jnp.int32)
        key_pos = first_row - margin + jnp.arange(5 * ROWS, dtype=jnp.int32)
        return attend(query_rows, query_pos, key_rows, value_rows, key_pos, utt_ends, FRAMES)
    context = lax.map(one_block, jnp.arange(N_SEQ, dtype=jnp.int32)).reshape(FRAMES, D)
    mixed = (residual_in.astype(jnp.float32) + context).astype(jnp.bfloat16)
    half_width = (KERNEL - 1) // 2
    mixed_padded = jnp.pad(mixed, ((half_width, half_width), (0, 0)))
    own_utt = utterance_ids(jnp.arange(FRAMES, dtype=jnp.int32), utt_ends, FRAMES)
    padded_utt = utterance_ids(jnp.arange(FRAMES + 2 * half_width, dtype=jnp.int32) - half_width, utt_ends, FRAMES)
    conv_sum = jnp.zeros((FRAMES, D), jnp.float32)
    for tap in range(KERNEL):
        same_utt = padded_utt[tap:tap + FRAMES] == own_utt
        term = mixed_padded[tap:tap + FRAMES].astype(jnp.float32) * depth_kernel[tap][None, :]
        conv_sum = conv_sum + jnp.where(same_utt[:, None], term, jnp.float32(0.0))
    mean_val = lax.optimization_barrier(jnp.mean(conv_sum, axis=1, keepdims=True))
    centred = conv_sum - mean_val
    var_val = lax.optimization_barrier(jnp.mean(centred * centred, axis=1, keepdims=True))
    normed = centred / jnp.sqrt(var_val + 1e-05) * norm_gain[None, :] + norm_shift[None, :]
    return (mixed.astype(jnp.float32) + normed * jax.nn.sigmoid(normed)).astype(jnp.bfloat16)
```

```python
import functools

import jax
import jax.numpy as jnp
from jax import lax
from jax.experimental import pallas as pl
from jax.experimental.pallas import tpu as pltpu
from jax.sharding import PartitionSpec as P

MESH = pl.DeviceIdType.MESH
HALO = 16
TILES = 2
CONV_ROWS = 64
NORM_ROWS = 32
WINDOW = 1536
APART = -4096.0


def block_kernel(
    n,
    lens_hbm,
    taps_hbm,
    gain_hbm,
    shift_hbm,
    q_hbm,
    k_hbm,
    v_hbm,
    r_hbm,
    out_ref,
    lens_ref,
    taps_ref,
    gain_ref,
    shift_ref,
    qb,
    rb,
    kv,
    pb,
    lens_pad,
    kf,
    qf,
    after,
    before,
    mx,
    cv,
    small_sem,
    local_sem,
    halo_send,
    halo_recv,
    send_sem,
    recv_sem,
):
    rows, width = q_hbm.shape
    kb, vb = kv.at[0], kv.at[1]
    n_chunks = width // 128
    span = 5 * rows
    q_rows = rows + 2 * HALO
    me = lax.axis_index("seq")
    par = me % 2
    partner = me + 1 - 2 * par
    up = (me + 2) % n
    down = (me + n - 2) % n
    cross = (me + n - 1 + 2 * par) % n

    small = [
        pltpu.make_async_copy(src, dst, small_sem.at[i])
        for i, (src, dst) in enumerate(
            (
                (lens_hbm, lens_ref),
                (taps_hbm, taps_ref),
                (gain_hbm, gain_ref),
                (shift_hbm, shift_ref),
            )
        )
    ]
    for copy in small:
        copy.start()
    own = [
        pltpu.make_async_copy(k_hbm, kb.at[pl.ds(2 * rows, rows)], local_sem.at[0]),
        pltpu.make_async_copy(v_hbm, vb.at[pl.ds(2 * rows, rows)], local_sem.at[1]),
        pltpu.make_async_copy(q_hbm, qb.at[pl.ds(HALO, rows)], local_sem.at[2]),
        pltpu.make_async_copy(r_hbm, rb.at[pl.ds(HALO, rows)], local_sem.at[3]),
    ]
    for copy in own:
        copy.start()

    barrier = pltpu.get_barrier_semaphore()
    for other in (partner, up, down, cross):
        pl.semaphore_signal(barrier, inc=1, device_id={"seq": other}, device_id_type=MESH)
    pl.semaphore_wait(barrier, 4)

    def remote(src, dst, ssem, rsem, other):
        return pltpu.make_async_remote_copy(
            src_ref=src,
            dst_ref=dst,
            send_sem=ssem,
            recv_sem=rsem,
            device_id={"seq": other},
            device_id_type=MESH,
        )

    last = rows - HALO
    halos = []
    for side, other, src_row, dst_row in (
        (0, partner, last * (1 - par), (rows + HALO) * par),
        (1, cross, last * par, (rows + HALO) * (1 - par)),
    ):
        for which, src, dst in ((0, q_hbm, qb), (1, r_hbm, rb)):
            halos.append(
                remote(
                    src.at[pl.ds(pl.multiple_of(src_row, HALO), HALO)],
                    dst.at[pl.ds(pl.multiple_of(dst_row, HALO), HALO)],
                    halo_send.at[side, which],
                    halo_recv.at[side, which],
                    other,
                )
            )

    def columns(c):
        return pl.ds(pl.multiple_of(c * 128, 128), 128)

    def place(row):
        return pl.ds(pl.multiple_of(row, 32), rows)

    def send(c, kind, which):
        cols = columns(c)
        dst = kv.at[which]
        src = None if kind == 3 or not isinstance(which, int) else (k_hbm, v_hbm)[which]
        src = kv.at[which, pl.ds(2 * rows, rows)] if src is None else src
        src = src.at[:, cols]
        if kind == 0:
            args = src, dst.at[pl.ds(0, rows), cols], up
        elif kind == 1:
            args = src, dst.at[pl.ds(4 * rows, rows), cols], down
        elif kind == 2:
            args = src, dst.at[place(rows + 2 * rows * par), cols], partner
        else:
            args = (
                dst.at[place(4 * rows * (1 - par)), cols],
                dst.at[place(3 * rows - 2 * rows * par), cols],
                partner,
            )
        return remote(
            args[0],
            args[1],
            send_sem.at[kind, c, which],
            recv_sem.at[kind, c, which],
            args[2],
        )

    for copy in halos:
        copy.start()

    for which in (0, 1):

        def start_chunk(c, carry, which=which):
            for kind in (0, 1, 2):
                send(c, kind, which).start()
            return carry

        lax.fori_loop(0, n_chunks, start_chunk, 0)

    for copy in small:
        copy.wait()
    lens_pad[...] = jnp.zeros(lens_pad.shape, jnp.float32)
    lens_pad[:, pl.ds(0, lens_ref.shape[1])] = lens_ref[...].astype(jnp.float32)
    lens = lens_pad[...]
    low = lax.broadcasted_iota(jnp.int32, (128, 128), 0)
    lane = lax.broadcasted_iota(jnp.int32, (128, 128), 1)
    wide = jnp.broadcast_to(lens, (128, 128))
    tall = jnp.sum(jnp.where(low == lane, wide, 0.0), axis=1, keepdims=True)
    ends = jnp.sum(jnp.where(low <= lane, tall, 0.0), axis=0, keepdims=True)
    starts = ends - lens

    def member(first, count):
        pos = first + lax.broadcasted_iota(jnp.int32, (count, 128), 0)
        pos = pos.astype(jnp.float32)
        return pos, (pos >= starts) & (pos < ends)

    base = me * rows
    for part in range(5):
        _, inside = member(base + (part - 2) * rows, rows)
        kf[pl.ds(part * rows, rows), :] = jnp.where(inside, 0.0, APART).astype(jnp.bfloat16)
    _, inside = member(base - HALO, q_rows)
    qf[...] = jnp.where(inside, 1.0, 0.0).astype(jnp.bfloat16)
    pos, inside = member(base, rows)
    first = jnp.sum(jnp.where(inside, starts, 0.0), axis=1, keepdims=True)
    final = jnp.sum(jnp.where(inside, ends, 0.0), axis=1, keepdims=True)
    before[...] = pos - first
    after[...] = final - 1.0 - pos

    for copy in own:
        copy.wait()
    for copy in halos:
        copy.wait_recv()

    tile = q_rows // TILES
    window = WINDOW
    even = lax.broadcasted_iota(jnp.int32, (tile, 128), 1) < 64
    is_even = (lax.broadcasted_iota(jnp.int32, (1, 128), 1) < 64).astype(jnp.float32)
    lo = is_even.astype(jnp.bfloat16)
    hi = (1.0 - is_even).astype(jnp.bfloat16)
    ones = jnp.ones((window, 128), jnp.bfloat16)

    mx[:, columns(0)] = jnp.zeros((q_rows, 128), jnp.float32)
    half = taps_ref.shape[0] // 2

    def weigh(c):
        cols = columns(c)
        for t in range(TILES):
            mine = pl.ds(t * tile, tile)
            keys = pl.ds(t * (span - window), window)
            qt = qb[mine, cols] * jnp.bfloat16(0.125)
            feat = qf[mine, :]
            q2 = jnp.concatenate(
                [
                    jnp.concatenate([qt * lo, feat], axis=1),
                    jnp.concatenate([qt * hi, feat], axis=1),
                ],
                axis=0,
            )
            kk = jnp.concatenate([kb[keys, cols], kf[keys, :]], axis=1)
            s = lax.dot_general(
                q2, kk, (((1,), (1,)), ((), ())), preferred_element_type=jnp.float32
            )
            m = jnp.max(s, axis=1, keepdims=True)
            pb[c * TILES + t] = jnp.exp(s - m).astype(jnp.bfloat16)

    def convolve(c):
        cols = columns(c)
        for r in range(0, rows, CONV_ROWS):
            some = pl.ds(r, CONV_ROWS)
            room_before = before[some, :]
            room_after = after[some, :]
            acc = jnp.zeros((CONV_ROWS, 128), jnp.float32)
            for j in range(2 * half + 1):
                by = j - half
                x = mx[pl.ds(r + HALO + by, CONV_ROWS), cols]
                if by < 0:
                    x = jnp.where(room_before >= float(-by), x, 0.0)
                elif by > 0:
                    x = jnp.where(room_after >= float(by), x, 0.0)
                acc = acc + x * taps_ref[pl.ds(j, 1), cols]
            cv[some, cols] = acc

    def mix(c):
        cols = columns(c)
        for t in range(TILES):
            mine = pl.ds(t * tile, tile)
            keys = pl.ds(t * (span - window), window)
            vv = jnp.concatenate([vb[keys, cols], ones], axis=1)
            o = jnp.dot(pb[c * TILES + t], vv, preferred_element_type=jnp.float32)
            num = jnp.where(even, o[:tile, :128], o[tile:, :128])
            den = jnp.where(even, o[:tile, 128:], o[tile:, 128:])
            mixed = rb[mine, cols].astype(jnp.float32) + num / den
            mx[mine, cols] = mixed.astype(jnp.bfloat16).astype(jnp.float32)

    def step(i, carry):
        @pl.when(i < 2 * n_chunks)
        def _():
            which, c = i // n_chunks, i % n_chunks
            for kind in (0, 1):
                send(c, kind, which).wait_recv()
            send(c, 3, which).start()

        @pl.when((i >= 1) & (i <= n_chunks))
        def _():
            for kind in (2, 3):
                send(i - 1, kind, 0).wait_recv()
            weigh(i - 1)

        @pl.when(i > n_chunks)
        def _():
            c = i - 1 - n_chunks
            for kind in (2, 3):
                send(c, kind, 1).wait_recv()
            convolve(lax.max(c - 1, 0))
            mix(c)

        return carry

    lax.fori_loop(0, 2 * n_chunks + 1, step, 0)
    convolve(n_chunks - 1)

    for r in range(0, rows, NORM_ROWS):
        some = pl.ds(r, NORM_ROWS)
        x = cv[some, :]
        mean = jnp.sum(x, axis=1, keepdims=True) * (1.0 / width)
        x = x - mean
        var = jnp.sum(x * x, axis=1, keepdims=True) * (1.0 / width)
        normed = x * lax.rsqrt(var + 1e-05) * gain_ref[...] + shift_ref[...]
        gated = 0.5 * normed
        gated = gated + gated * jnp.tanh(gated)
        result = mx[pl.ds(r + HALO, NORM_ROWS), :] + gated
        out_ref[some, :] = result.astype(out_ref.dtype)

    for copy in halos:
        copy.wait_send()

    def finish(c, carry):
        for kind in range(4):
            for which in (0, 1):
                send(c, kind, which).wait_send()
        return carry

    lax.fori_loop(0, n_chunks, finish, 0)


def local(
    query_proj,
    key_proj,
    value_proj,
    residual_in,
    utter_lengths,
    depth_kernel,
    norm_gain,
    norm_shift,
):
    rows, width = query_proj.shape
    n = lax.axis_size("seq")
    n_chunks = width // 128
    q_rows, span = rows + 2 * HALO, 5 * rows
    vmem = pl.BlockSpec(memory_space=pltpu.VMEM)
    hbm = pl.BlockSpec(memory_space=pltpu.HBM)
    bf16, f32 = jnp.bfloat16, jnp.float32
    return pl.pallas_call(
        functools.partial(block_kernel, n),
        out_shape=jax.ShapeDtypeStruct((rows, width), bf16),
        in_specs=[hbm] * 8,
        out_specs=vmem,
        scratch_shapes=[
            pltpu.VMEM((1, utter_lengths.shape[0]), jnp.int32),
            pltpu.VMEM(depth_kernel.shape, f32),
            pltpu.VMEM((1, width), f32),
            pltpu.VMEM((1, width), f32),
            pltpu.VMEM((q_rows, width), bf16),
            pltpu.VMEM((q_rows, width), bf16),
            pltpu.VMEM((2, span, width), bf16),
            pltpu.VMEM((TILES * n_chunks, 2 * q_rows // TILES, WINDOW), bf16),
            pltpu.VMEM((1, 128), f32),
            pltpu.VMEM((span, 128), bf16),
            pltpu.VMEM((q_rows, 128), bf16),
            pltpu.VMEM((rows, 128), f32),
            pltpu.VMEM((rows, 128), f32),
            pltpu.VMEM((q_rows, width), f32),
            pltpu.VMEM((rows, width), f32),
            pltpu.SemaphoreType.DMA((4,)),
            pltpu.SemaphoreType.DMA((4,)),
            pltpu.SemaphoreType.DMA((2, 2)),
            pltpu.SemaphoreType.DMA((2, 2)),
            pltpu.SemaphoreType.DMA((4, n_chunks, 2)),
            pltpu.SemaphoreType.DMA((4, n_chunks, 2)),
        ],
        compiler_params=pltpu.CompilerParams(
            collective_id=0, has_side_effects=True, vmem_limit_bytes=44 << 20
        ),
        name="conformer_block",
    )(
        *(
            pltpu.with_memory_space_constraint(array, pltpu.HBM)
            for array in (
                utter_lengths.reshape(1, -1),
                depth_kernel,
                norm_gain.reshape(1, -1),
                norm_shift.reshape(1, -1),
                query_proj,
                key_proj,
                value_proj,
                residual_in,
            )
        )
    )


def solution(mesh):
    return jax.shard_map(
        local,
        mesh=mesh,
        in_specs=(
            P(("dp", "seq"), None),
            P(("dp", "seq"), None),
            P(("dp", "seq"), None),
            P(("dp", "seq"), None),
            P("dp"),
            P(),
            P(),
            P(),
        ),
        out_specs=P(("dp", "seq"), None),
        check_vma=False,
    )
```

```python
import functools

import jax
import jax.numpy as jnp
from jax import lax
from jax.experimental import pallas as pl
from jax.experimental.pallas import tpu as pltpu
from jax.sharding import PartitionSpec as P

MESH = pl.DeviceIdType.MESH
HALO = 16
TILES = 2
CONV_ROWS = 64
NORM_ROWS = 32
WINDOW = 1536
APART = -4096.0


def block_kernel(
    n,
    lens_hbm,
    taps_hbm,
    gain_hbm,
    shift_hbm,
    q_hbm,
    k_hbm,
    v_hbm,
    r_hbm,
    out_ref,
    lens_ref,
    taps_ref,
    gain_ref,
    shift_ref,
    passing,
    qb,
    rb,
    kv,
    pb,
    lens_pad,
    kf,
    qf,
    after,
    before,
    mxs,
    cvs,
    mb,
    cv,
    small_sem,
    local_sem,
    halo_send,
    halo_recv,
    send_sem,
    recv_sem,
):
    rows, width = q_hbm.shape
    kb, vb = kv.at[0], kv.at[1]
    n_chunks = width // 128
    span = 5 * rows
    q_rows = rows + 2 * HALO
    me = lax.axis_index("seq")
    par = me % 2
    partner = me + 1 - 2 * par
    near = (me + n - 2 + 4 * par) % n
    far = (me + n + 2 - 4 * par) % n

    small = [
        pltpu.make_async_copy(src, dst, small_sem.at[i])
        for i, (src, dst) in enumerate(
            (
                (lens_hbm, lens_ref),
                (taps_hbm, taps_ref),
                (gain_hbm, gain_ref),
                (shift_hbm, shift_ref),
            )
        )
    ]
    for copy in small:
        copy.start()
    own = [
        pltpu.make_async_copy(k_hbm, kb.at[pl.ds(2 * rows, rows)], local_sem.at[0]),
        pltpu.make_async_copy(v_hbm, vb.at[pl.ds(2 * rows, rows)], local_sem.at[1]),
        pltpu.make_async_copy(q_hbm, qb.at[pl.ds(HALO, rows)], local_sem.at[2]),
        pltpu.make_async_copy(r_hbm, rb.at[pl.ds(HALO, rows)], local_sem.at[3]),
    ]
    for copy in own:
        copy.start()

    barrier = pltpu.get_barrier_semaphore()
    for other in (partner, near, far):
        pl.semaphore_signal(barrier, inc=1, device_id={"seq": other}, device_id_type=MESH)
    pl.semaphore_wait(barrier, 3)

    def remote(src, dst, ssem, rsem, other):
        return pltpu.make_async_remote_copy(
            src_ref=src,
            dst_ref=dst,
            send_sem=ssem,
            recv_sem=rsem,
            device_id={"seq": other},
            device_id_type=MESH,
        )

    last = rows - HALO

    def edge(row):
        return pl.ds(pl.multiple_of(row, HALO), HALO)

    halos = []
    for which, src, dst in ((0, q_hbm, qb), (1, r_hbm, rb)):
        ends = (
            (src.at[edge(last * (1 - par))], dst.at[edge((rows + HALO) * par)], partner),
            (src.at[edge(last * par)], passing.at[which], partner),
            (passing.at[which], dst.at[edge((rows + HALO) * par)], far),
        )
        halos.append(
            [
                remote(*ends[kind][:2], halo_send.at[kind, which], halo_recv.at[kind, which], ends[kind][2])
                for kind in range(3)
            ]
        )

    def columns(c):
        return pl.ds(pl.multiple_of(c * 128, 128), 128)

    def place(row):
        return pl.ds(pl.multiple_of(row, 32), rows)

    def send(c, kind, which):
        cols = columns(c)
        dst = kv.at[which]
        src = None if kind == 3 or not isinstance(which, int) else (k_hbm, v_hbm)[which]
        src = kv.at[which, pl.ds(2 * rows, rows)] if src is None else src
        src = src.at[:, cols]
        if kind == 0:
            args = src, dst.at[place(4 * rows * (1 - par)), cols], near
        elif kind == 1:
            args = src, dst.at[place(4 * rows * par), cols], far
        elif kind == 2:
            args = src, dst.at[place(rows + 2 * rows * par), cols], partner
        else:
            args = (
                dst.at[place(4 * rows * (1 - par)), cols],
                dst.at[place(3 * rows - 2 * rows * par), cols],
                partner,
            )
        return remote(
            args[0],
            args[1],
            send_sem.at[kind, c, which],
            recv_sem.at[kind, c, which],
            args[2],
        )

    for kind in (1, 0):
        for pair in halos:
            pair[kind].start()

    def begin(kinds, which):
        def start_chunk(c, carry):
            for kind in kinds:
                send(c, kind, which).start()
            return carry

        lax.fori_loop(0, n_chunks, start_chunk, 0)

    begin((0, 2), 0)
    for pair in halos:
        pair[1].wait_recv()
        pair[2].start()
    begin((1,), 0)
    begin((0, 2), 1)
    begin((1,), 1)

    for copy in small:
        copy.wait()
    lens_pad[...] = jnp.zeros(lens_pad.shape, jnp.float32)
    lens_pad[:, pl.ds(0, lens_ref.shape[1])] = lens_ref[...].astype(jnp.float32)
    lens = lens_pad[...]
    low = lax.broadcasted_iota(jnp.int32, (128, 128), 0)
    lane = lax.broadcasted_iota(jnp.int32, (128, 128), 1)
    wide = jnp.broadcast_to(lens, (128, 128))
    tall = jnp.sum(jnp.where(low == lane, wide, 0.0), axis=1, keepdims=True)
    ends = jnp.sum(jnp.where(low <= lane, tall, 0.0), axis=0, keepdims=True)
    starts = ends - lens

    def member(first, count):
        pos = first + lax.broadcasted_iota(jnp.int32, (count, 128), 0)
        pos = pos.astype(jnp.float32)
        return pos, (pos >= starts) & (pos < ends)

    base = me * rows
    for part in range(5):
        _, inside = member(base + (part - 2) * rows, rows)
        kf[pl.ds(part * rows, rows), :] = jnp.where(inside, 0.0, APART).astype(jnp.bfloat16)
    _, inside = member(base - HALO, q_rows)
    qf[...] = jnp.where(inside, 1.0, 0.0).astype(jnp.bfloat16)
    pos, inside = member(base, rows)
    first = jnp.sum(jnp.where(inside, starts, 0.0), axis=1, keepdims=True)
    final = jnp.sum(jnp.where(inside, ends, 0.0), axis=1, keepdims=True)
    before[...] = pos - first
    after[...] = final - 1.0 - pos

    for copy in own:
        copy.wait()
    for pair in halos:
        pair[0].wait_recv()
        pair[2].wait_recv()

    tile = q_rows // TILES
    window = WINDOW
    even = lax.broadcasted_iota(jnp.int32, (tile, 128), 1) < 64
    is_even = (lax.broadcasted_iota(jnp.int32, (1, 128), 1) < 64).astype(jnp.float32)
    lo = is_even.astype(jnp.bfloat16)
    hi = (1.0 - is_even).astype(jnp.bfloat16)
    ones = jnp.ones((window, 128), jnp.bfloat16)

    mxs[1] = jnp.zeros((q_rows, 128), jnp.float32)
    half = taps_ref.shape[0] // 2

    def weigh(c):
        cols = columns(c)
        for t in range(TILES):
            mine = pl.ds(t * tile, tile)
            keys = pl.ds(t * (span - window), window)
            qt = qb[mine, cols] * jnp.bfloat16(0.125)
            feat = qf[mine, :]
            q2 = jnp.concatenate(
                [
                    jnp.concatenate([qt * lo, feat], axis=1),
                    jnp.concatenate([qt * hi, feat], axis=1),
                ],
                axis=0,
            )
            kk = jnp.concatenate([kb[keys, cols], kf[keys, :]], axis=1)
            s = lax.dot_general(
                q2, kk, (((1,), (1,)), ((), ())), preferred_element_type=jnp.float32
            )
            m = jnp.max(s, axis=1, keepdims=True)
            pb[c * TILES + t] = jnp.exp(s - m).astype(jnp.bfloat16)

    def convolve(c, mx, cv):
        cols = columns(c)
        for r in range(0, rows, CONV_ROWS):
            some = pl.ds(r, CONV_ROWS)
            room_before = before[some, :]
            room_after = after[some, :]
            acc = jnp.zeros((CONV_ROWS, 128), jnp.float32)
            for j in range(2 * half + 1):
                by = j - half
                x = mx[pl.ds(r + HALO + by, CONV_ROWS), :]
                if by < 0:
                    x = jnp.where(room_before >= float(-by), x, 0.0)
                elif by > 0:
                    x = jnp.where(room_after >= float(by), x, 0.0)
                acc = acc + x * taps_ref[pl.ds(j, 1), cols]
            cv[some, cols] = acc

    def mix(c, mx):
        cols = columns(c)
        for t in range(TILES):
            mine = pl.ds(t * tile, tile)
            keys = pl.ds(t * (span - window), window)
            vv = jnp.concatenate([vb[keys, cols], ones], axis=1)
            o = jnp.dot(pb[c * TILES + t], vv, preferred_element_type=jnp.float32)
            num = jnp.where(even, o[:tile, :128], o[tile:, :128])
            den = jnp.where(even, o[:tile, 128:], o[tile:, 128:])
            mixed = rb[mine, cols].astype(jnp.float32) + num / den
            mx[mine, :] = mixed.astype(jnp.bfloat16).astype(jnp.float32)

    def take(i):
        which, c = i // n_chunks, i % n_chunks
        send(c, 0, which).wait_recv()
        send(c, 3, which).start()

    def ready(c, which):
        for kind in (2, 3, 1):
            send(c, kind, which).wait_recv()

    take(0)

    def weigh_step(c, carry):
        take(c + 1)
        ready(c, 0)
        weigh(c)
        return carry

    lax.fori_loop(0, n_chunks, weigh_step, 0)

    def keep(c, a):
        cols = columns(c)
        mb[:, cols] = mxs[a, pl.ds(HALO, rows), :].astype(jnp.bfloat16)

    def mix_step(j, carry):
        for a in (0, 1):
            c = 2 * j + a
            prev = lax.max(c - 1, 0)
            convolve(prev, mxs.at[1 - a], cv)

            @pl.when(c + 1 < n_chunks)
            def _():
                take(n_chunks + c + 1)

            ready(c, 1)
            mix(c, mxs.at[a])
            keep(c, a)
        return carry

    lax.fori_loop(0, n_chunks // 2, mix_step, 0)
    convolve(n_chunks - 1, mxs.at[1], cv)

    for r in range(0, rows, NORM_ROWS):
        some = pl.ds(r, NORM_ROWS)
        x = cv[some, :]
        mean = jnp.sum(x, axis=1, keepdims=True) * (1.0 / width)
        x = x - mean
        var = jnp.sum(x * x, axis=1, keepdims=True) * (1.0 / width)
        normed = x * lax.rsqrt(var + 1e-05) * gain_ref[...] + shift_ref[...]
        gated = 0.5 * normed
        gated = gated + gated * jnp.tanh(gated)
        result = mb[some, :].astype(jnp.float32) + gated
        out_ref[some, :] = result.astype(out_ref.dtype)

    for pair in halos:
        for copy in pair:
            copy.wait_send()

    def finish(c, carry):
        for kind in range(4):
            for which in (0, 1):
                send(c, kind, which).wait_send()
        return carry

    lax.fori_loop(0, n_chunks, finish, 0)


def local(
    query_proj,
    key_proj,
    value_proj,
    residual_in,
    utter_lengths,
    depth_kernel,
    norm_gain,
    norm_shift,
):
    rows, width = query_proj.shape
    n = lax.axis_size("seq")
    n_chunks = width // 128
    q_rows, span = rows + 2 * HALO, 5 * rows
    vmem = pl.BlockSpec(memory_space=pltpu.VMEM)
    hbm = pl.BlockSpec(memory_space=pltpu.HBM)
    bf16, f32 = jnp.bfloat16, jnp.float32
    return pl.pallas_call(
        functools.partial(block_kernel, n),
        out_shape=jax.ShapeDtypeStruct((rows, width), bf16),
        in_specs=[hbm] * 8,
        out_specs=vmem,
        scratch_shapes=[
            pltpu.VMEM((1, utter_lengths.shape[0]), jnp.int32),
            pltpu.VMEM(depth_kernel.shape, f32),
            pltpu.VMEM((1, width), f32),
            pltpu.VMEM((1, width), f32),
            pltpu.VMEM((2, HALO, width), bf16),
            pltpu.VMEM((q_rows, width), bf16),
            pltpu.VMEM((q_rows, width), bf16),
            pltpu.VMEM((2, span, width), bf16),
            pltpu.VMEM((TILES * n_chunks, 2 * q_rows // TILES, WINDOW), bf16),
            pltpu.VMEM((1, 128), f32),
            pltpu.VMEM((span, 128), bf16),
            pltpu.VMEM((q_rows, 128), bf16),
            pltpu.VMEM((rows, 128), f32),
            pltpu.VMEM((rows, 128), f32),
            pltpu.VMEM((2, q_rows, 128), f32),
            pltpu.VMEM((rows, 128), f32),
            pltpu.VMEM((rows, width), bf16),
            pltpu.VMEM((rows, width), f32),
            pltpu.SemaphoreType.DMA((4,)),
            pltpu.SemaphoreType.DMA((4,)),
            pltpu.SemaphoreType.DMA((3, 2)),
            pltpu.SemaphoreType.DMA((3, 2)),
            pltpu.SemaphoreType.DMA((4, n_chunks, 2)),
            pltpu.SemaphoreType.DMA((4, n_chunks, 2)),
        ],
        compiler_params=pltpu.CompilerParams(
            collective_id=0, has_side_effects=True, vmem_limit_bytes=44 << 20
        ),
        name="conformer_block",
    )(
        *(
            pltpu.with_memory_space_constraint(array, pltpu.HBM)
            for array in (
                utter_lengths.reshape(1, -1),
                depth_kernel,
                norm_gain.reshape(1, -1),
                norm_shift.reshape(1, -1),
                query_proj,
                key_proj,
                value_proj,
                residual_in,
            )
        )
    )


def solution(mesh):
    return jax.shard_map(
        local,
        mesh=mesh,
        in_specs=(
            P(("dp", "seq"), None),
            P(("dp", "seq"), None),
            P(("dp", "seq"), None),
            P(("dp", "seq"), None),
            P("dp"),
            P(),
            P(),
            P(),
        ),
        out_specs=P(("dp", "seq"), None),
        check_vma=False,
    )
```

```python
import functools

import jax
import jax.numpy as jnp
from jax import lax
from jax.experimental import pallas as pl
from jax.experimental.pallas import tpu as pltpu
from jax.sharding import PartitionSpec as P

MESH = pl.DeviceIdType.MESH
HALO = 16
TILES = 2
CONV_ROWS = 64
NORM_ROWS = 32
WINDOW = 1536
AHEAD = 1
APART = -4096.0


def block_kernel(
    n,
    lens_hbm,
    taps_hbm,
    gain_hbm,
    shift_hbm,
    q_hbm,
    k_hbm,
    v_hbm,
    r_hbm,
    out_ref,
    lens_ref,
    taps_ref,
    gain_ref,
    shift_ref,
    passing,
    qb,
    rb,
    kv,
    pb,
    lens_pad,
    kf,
    qf,
    after,
    before,
    keeps,
    lag,
    mxs,
    mb,
    cv,
    small_sem,
    local_sem,
    halo_send,
    halo_recv,
    send_sem,
    recv_sem,
):
    rows, width = q_hbm.shape
    kb, vb = kv.at[0], kv.at[1]
    n_chunks = width // 128
    span = 5 * rows
    q_rows = rows + 2 * HALO
    me = lax.axis_index("seq")
    par = me % 2
    partner = me + 1 - 2 * par
    near = (me + n - 2 + 4 * par) % n
    far = (me + n + 2 - 4 * par) % n

    barrier = pltpu.get_barrier_semaphore()
    for other in (partner, near, far):
        pl.semaphore_signal(barrier, inc=1, device_id={"seq": other}, device_id_type=MESH)

    small = [
        pltpu.make_async_copy(src, dst, small_sem.at[i])
        for i, (src, dst) in enumerate(
            (
                (lens_hbm, lens_ref),
                (taps_hbm, taps_ref),
                (gain_hbm, gain_ref),
                (shift_hbm, shift_ref),
            )
        )
    ]
    for copy in small:
        copy.start()
    own = [
        pltpu.make_async_copy(k_hbm, kb.at[pl.ds(2 * rows, rows)], local_sem.at[0]),
        pltpu.make_async_copy(v_hbm, vb.at[pl.ds(2 * rows, rows)], local_sem.at[1]),
        pltpu.make_async_copy(q_hbm, qb.at[pl.ds(HALO, rows)], local_sem.at[2]),
        pltpu.make_async_copy(r_hbm, rb.at[pl.ds(HALO, rows)], local_sem.at[3]),
    ]
    for copy in own:
        copy.start()

    pl.semaphore_wait(barrier, 3)

    def remote(src, dst, ssem, rsem, other):
        return pltpu.make_async_remote_copy(
            src_ref=src,
            dst_ref=dst,
            send_sem=ssem,
            recv_sem=rsem,
            device_id={"seq": other},
            device_id_type=MESH,
        )

    last = rows - HALO

    def edge(row):
        return pl.ds(pl.multiple_of(row, HALO), HALO)

    halos = []
    for which, src, dst in ((0, q_hbm, qb), (1, r_hbm, rb)):
        ends = (
            (src.at[edge(last * (1 - par))], dst.at[edge((rows + HALO) * par)], partner),
            (src.at[edge(last * par)], passing.at[which], partner),
            (passing.at[which], dst.at[edge((rows + HALO) * par)], far),
        )
        halos.append(
            [
                remote(*ends[kind][:2], halo_send.at[kind, which], halo_recv.at[kind, which], ends[kind][2])
                for kind in range(3)
            ]
        )

    def columns(c):
        return pl.ds(pl.multiple_of(c * 128, 128), 128)

    def place(row):
        return pl.ds(pl.multiple_of(row, 32), rows)

    def send(c, kind, which):
        cols = columns(c)
        dst = kv.at[which]
        src = None if kind == 3 or not isinstance(which, int) else (k_hbm, v_hbm)[which]
        src = kv.at[which, pl.ds(2 * rows, rows)] if src is None else src
        src = src.at[:, cols]
        if kind == 0:
            args = src, dst.at[place(4 * rows * (1 - par)), cols], near
        elif kind == 1:
            args = src, dst.at[place(4 * rows * par), cols], far
        elif kind == 2:
            args = src, dst.at[place(rows + 2 * rows * par), cols], partner
        else:
            args = (
                dst.at[place(4 * rows * (1 - par)), cols],
                dst.at[place(3 * rows - 2 * rows * par), cols],
                partner,
            )
        return remote(
            args[0],
            args[1],
            send_sem.at[kind, c, which],
            recv_sem.at[kind, c, which],
            args[2],
        )

    def begin(kinds, which, first=0):
        def start_chunk(c, carry):
            for kind in kinds:
                send(c, kind, which).start()
            return carry

        lax.fori_loop(first, n_chunks, start_chunk, 0)

    for c in range(AHEAD):
        send(c, 0, 0).start()
        send(c, 1, 0).start()
    for kind in (1, 0):
        for pair in halos:
            pair[kind].start()
    begin((0,), 0, AHEAD)
    begin((2,), 0)
    for pair in halos:
        pair[1].wait_recv()
        pair[2].start()
    begin((1,), 0, AHEAD)
    begin((0, 2), 1)
    begin((1,), 1)

    for copy in small:
        copy.wait()
    lens_pad[...] = jnp.zeros(lens_pad.shape, jnp.float32)
    lens_pad[:, pl.ds(0, lens_ref.shape[1])] = lens_ref[...].astype(jnp.float32)
    lens = lens_pad[...]
    low = lax.broadcasted_iota(jnp.int32, (128, 128), 0)
    lane = lax.broadcasted_iota(jnp.int32, (128, 128), 1)
    wide = jnp.broadcast_to(lens, (128, 128))
    tall = jnp.sum(jnp.where(low == lane, wide, 0.0), axis=1, keepdims=True)
    ends = jnp.sum(jnp.where(low <= lane, tall, 0.0), axis=0, keepdims=True)
    starts = ends - lens

    def member(first, count):
        pos = first + lax.broadcasted_iota(jnp.int32, (count, 128), 0)
        pos = pos.astype(jnp.float32)
        return pos, (pos >= starts) & (pos < ends)

    base = me * rows
    for part in range(5):
        _, inside = member(base + (part - 2) * rows, rows)
        kf[pl.ds(part * rows, rows), :] = jnp.where(inside, 0.0, APART).astype(jnp.bfloat16)
    _, inside = member(base - HALO, q_rows)
    qf[...] = jnp.where(inside, 1.0, 0.0).astype(jnp.bfloat16)
    pos, inside = member(base, rows)
    first = jnp.sum(jnp.where(inside, starts, 0.0), axis=1, keepdims=True)
    final = jnp.sum(jnp.where(inside, ends, 0.0), axis=1, keepdims=True)
    shifted = rows + 8
    half = taps_ref.shape[0] // 2
    for room, value in ((before, pos - first), (after, final - 1.0 - pos)):
        room[pl.ds(0, 8), :] = jnp.full((8, 128), -1.0, jnp.float32)
        room[pl.ds(shifted, 8), :] = jnp.full((8, 128), -1.0, jnp.float32)
        room[pl.ds(8, rows), :] = jnp.broadcast_to(value, (rows, 128))
    for j in range(2 * half + 1):
        if j != half:
            room = before if j < half else after
            near_rows = room[pl.ds(8 - (j + 1) % 8, shifted), :]
            keeps[j] = jnp.where(near_rows >= float(abs(j - half)), 1.0, 0.0)

    for copy in own:
        copy.wait()
    for pair in halos:
        pair[0].wait_recv()
        pair[2].wait_recv()

    tile = q_rows // TILES
    window = WINDOW
    even = lax.broadcasted_iota(jnp.int32, (tile, 128), 1) < 64
    is_even = (lax.broadcasted_iota(jnp.int32, (1, 128), 1) < 64).astype(jnp.float32)
    lo = is_even.astype(jnp.bfloat16)
    hi = (1.0 - is_even).astype(jnp.bfloat16)
    ones = jnp.ones((window, 128), jnp.bfloat16)

    mxs[1] = jnp.zeros((q_rows, 128), jnp.float32)
    def weigh(c):
        cols = columns(c)
        for t in range(TILES):
            mine = pl.ds(t * tile, tile)
            keys = pl.ds(t * (span - window), window)
            qt = qb[mine, cols] * jnp.bfloat16(0.125)
            feat = qf[mine, :]
            q2 = jnp.concatenate(
                [
                    jnp.concatenate([qt * lo, feat], axis=1),
                    jnp.concatenate([qt * hi, feat], axis=1),
                ],
                axis=0,
            )
            kk = jnp.concatenate([kb[keys, cols], kf[keys, :]], axis=1)
            s = lax.dot_general(
                q2, kk, (((1,), (1,)), ((), ())), preferred_element_type=jnp.float32
            )
            m = jnp.max(s, axis=1, keepdims=True)
            pb[c * TILES + t] = jnp.exp(s - m).astype(jnp.bfloat16)

    def convolve(c, mx, cv):
        cols = columns(c)
        for y in range(0, shifted, CONV_ROWS):
            count = min(CONV_ROWS, shifted - y)
            for r in range(8):
                acc = None
                for j in range(taps_ref.shape[0]):
                    if (j + 1) % 8 == r:
                        x = mx[pl.ds(y + j + 1 - r, count), :]
                        if j != half:
                            x = x * keeps[j, pl.ds(y, count), :]
                        x = x * taps_ref[pl.ds(j, 1), cols]
                        acc = x if acc is None else acc + x
                lag[r, pl.ds(y, count), :] = acc
        for t in range(0, rows, CONV_ROWS):
            acc = lag[0, pl.ds(t, CONV_ROWS), :]
            for r in range(1, 8):
                acc = acc + lag[r, pl.ds(t + r, CONV_ROWS), :]
            cv[pl.ds(t, CONV_ROWS), cols] = acc

    def mix(c, mx):
        cols = columns(c)
        for t in range(TILES):
            mine = pl.ds(t * tile, tile)
            keys = pl.ds(t * (span - window), window)
            vv = jnp.concatenate([vb[keys, cols], ones], axis=1)
            o = jnp.dot(pb[c * TILES + t], vv, preferred_element_type=jnp.float32)
            num = jnp.where(even, o[:tile, :128], o[tile:, :128])
            den = jnp.where(even, o[:tile, 128:], o[tile:, 128:])
            mixed = rb[mine, cols].astype(jnp.float32) + num / den
            mx[mine, :] = mixed.astype(jnp.bfloat16).astype(jnp.float32)

    def take(i):
        which, c = i // n_chunks, i % n_chunks
        send(c, 0, which).wait_recv()
        send(c, 3, which).start()

    def ready(c, which):
        for kind in (2, 3, 1):
            send(c, kind, which).wait_recv()

    take(0)

    def weigh_step(c, carry):
        take(c + 1)
        ready(c, 0)
        weigh(c)
        return carry

    lax.fori_loop(0, n_chunks, weigh_step, 0)

    for pair in halos:
        for copy in pair:
            copy.wait_send()

    def keep(c, a):
        cols = columns(c)
        mb[:, cols] = mxs[a, pl.ds(HALO, rows), :].astype(jnp.bfloat16)

    def mix_step(j, carry):
        for a in (0, 1):
            c = 2 * j + a
            prev = lax.max(c - 1, 0)
            convolve(prev, mxs.at[1 - a], cv)

            @pl.when(c + 1 < n_chunks)
            def _():
                take(n_chunks + c + 1)

            ready(c, 1)
            mix(c, mxs.at[a])
            keep(c, a)
            for kind in range(4):
                send(c, kind, 0).wait_send()

            @pl.when(c > 0)
            def _():
                for kind in range(4):
                    send(c - 1, kind, 1).wait_send()

        return carry

    lax.fori_loop(0, n_chunks // 2, mix_step, 0)
    convolve(n_chunks - 1, mxs.at[1], cv)

    for r in range(0, rows, NORM_ROWS):
        some = pl.ds(r, NORM_ROWS)
        x = cv[some, :]
        mean = jnp.sum(x, axis=1, keepdims=True) * (1.0 / width)
        x = x - mean
        var = jnp.sum(x * x, axis=1, keepdims=True) * (1.0 / width)
        normed = x * lax.rsqrt(var + 1e-05) * gain_ref[...] + shift_ref[...]
        gated = 0.5 * normed
        gated = gated + gated * jnp.tanh(gated)
        result = mb[some, :].astype(jnp.float32) + gated
        out_ref[some, :] = result.astype(out_ref.dtype)

    for kind in range(4):
        send(n_chunks - 1, kind, 1).wait_send()


def local(
    query_proj,
    key_proj,
    value_proj,
    residual_in,
    utter_lengths,
    depth_kernel,
    norm_gain,
    norm_shift,
):
    rows, width = query_proj.shape
    n = lax.axis_size("seq")
    n_chunks = width // 128
    q_rows, span = rows + 2 * HALO, 5 * rows
    vmem = pl.BlockSpec(memory_space=pltpu.VMEM)
    hbm = pl.BlockSpec(memory_space=pltpu.HBM)
    bf16, f32 = jnp.bfloat16, jnp.float32
    return pl.pallas_call(
        functools.partial(block_kernel, n),
        out_shape=jax.ShapeDtypeStruct((rows, width), bf16),
        in_specs=[hbm] * 8,
        out_specs=vmem,
        scratch_shapes=[
            pltpu.VMEM((1, utter_lengths.shape[0]), jnp.int32),
            pltpu.VMEM(depth_kernel.shape, f32),
            pltpu.VMEM((1, width), f32),
            pltpu.VMEM((1, width), f32),
            pltpu.VMEM((2, HALO, width), bf16),
            pltpu.VMEM((q_rows, width), bf16),
            pltpu.VMEM((q_rows, width), bf16),
            pltpu.VMEM((2, span, width), bf16),
            pltpu.VMEM((TILES * n_chunks, 2 * q_rows // TILES, WINDOW), bf16),
            pltpu.VMEM((1, 128), f32),
            pltpu.VMEM((span, 128), bf16),
            pltpu.VMEM((q_rows, 128), bf16),
            pltpu.VMEM((rows + 16, 128), f32),
            pltpu.VMEM((rows + 16, 128), f32),
            pltpu.VMEM((depth_kernel.shape[0], rows + 8, 128), f32),
            pltpu.VMEM((8, rows + 8, 128), f32),
            pltpu.VMEM((2, q_rows, 128), f32),
            pltpu.VMEM((rows, width), bf16),
            pltpu.VMEM((rows, width), f32),
            pltpu.SemaphoreType.DMA((4,)),
            pltpu.SemaphoreType.DMA((4,)),
            pltpu.SemaphoreType.DMA((3, 2)),
            pltpu.SemaphoreType.DMA((3, 2)),
            pltpu.SemaphoreType.DMA((4, n_chunks, 2)),
            pltpu.SemaphoreType.DMA((4, n_chunks, 2)),
        ],
        compiler_params=pltpu.CompilerParams(
            collective_id=0, has_side_effects=True, vmem_limit_bytes=44 << 20
        ),
        name="conformer_block",
    )(
        *(
            pltpu.with_memory_space_constraint(array, pltpu.HBM)
            for array in (
                utter_lengths.reshape(1, -1),
                depth_kernel,
                norm_gain.reshape(1, -1),
                norm_shift.reshape(1, -1),
                query_proj,
                key_proj,
                value_proj,
                residual_in,
            )
        )
    )


def solution(mesh):
    return jax.shard_map(
        local,
        mesh=mesh,
        in_specs=(
            P(("dp", "seq"), None),
            P(("dp", "seq"), None),
            P(("dp", "seq"), None),
            P(("dp", "seq"), None),
            P("dp"),
            P(),
            P(),
            P(),
        ),
        out_specs=P(("dp", "seq"), None),
        check_vma=False,
    )
```

```python
import functools

import jax
import jax.numpy as jnp
from jax import lax
from jax.experimental import pallas as pl
from jax.experimental.pallas import tpu as pltpu
from jax.sharding import PartitionSpec as P

MESH = pl.DeviceIdType.MESH
HALO = 16
TILES = 2
CONV_ROWS = 64
NORM_ROWS = 16
WINDOW = 1536
AHEAD = 2
APART = -4096.0


def block_kernel(
    n,
    lens_hbm,
    taps_hbm,
    gain_hbm,
    shift_hbm,
    q_hbm,
    k_hbm,
    v_hbm,
    r_hbm,
    out_ref,
    lens_ref,
    taps_ref,
    gain_ref,
    shift_ref,
    passing,
    qb,
    rb,
    kv,
    pb,
    lens_pad,
    kf,
    qf,
    after,
    before,
    keeps,
    lag,
    mxs,
    mb,
    cv,
    small_sem,
    local_sem,
    halo_send,
    halo_recv,
    send_sem,
    recv_sem,
):
    rows, width = q_hbm.shape
    kb, vb = kv.at[0], kv.at[1]
    n_chunks = width // 128
    span = 5 * rows
    q_rows = rows + 2 * HALO
    me = lax.axis_index("seq")
    par = me % 2
    partner = me + 1 - 2 * par
    near = (me + n - 2 + 4 * par) % n
    far = (me + n + 2 - 4 * par) % n

    barrier = pltpu.get_barrier_semaphore()
    for other in (partner, near, far):
        pl.semaphore_signal(barrier, inc=1, device_id={"seq": other}, device_id_type=MESH)

    small = [
        pltpu.make_async_copy(src, dst, small_sem.at[i])
        for i, (src, dst) in enumerate(
            (
                (lens_hbm, lens_ref),
                (taps_hbm, taps_ref),
                (gain_hbm, gain_ref),
                (shift_hbm, shift_ref),
            )
        )
    ]
    for copy in small:
        copy.start()
    own = [
        pltpu.make_async_copy(k_hbm, kb.at[pl.ds(2 * rows, rows)], local_sem.at[0]),
        pltpu.make_async_copy(v_hbm, vb.at[pl.ds(2 * rows, rows)], local_sem.at[1]),
        pltpu.make_async_copy(q_hbm, qb.at[pl.ds(HALO, rows)], local_sem.at[2]),
        pltpu.make_async_copy(r_hbm, rb.at[pl.ds(HALO, rows)], local_sem.at[3]),
    ]
    for copy in own:
        copy.start()

    pl.semaphore_wait(barrier, 3)

    def remote(src, dst, ssem, rsem, other):
        return pltpu.make_async_remote_copy(
            src_ref=src,
            dst_ref=dst,
            send_sem=ssem,
            recv_sem=rsem,
            device_id={"seq": other},
            device_id_type=MESH,
        )

    last = rows - HALO

    def edge(row):
        return pl.ds(pl.multiple_of(row, HALO), HALO)

    halos = []
    for which, src, dst in ((0, q_hbm, qb), (1, r_hbm, rb)):
        ends = (
            (src.at[edge(last * (1 - par))], dst.at[edge((rows + HALO) * par)], partner),
            (src.at[edge(last * par)], passing.at[which], partner),
            (passing.at[which], dst.at[edge((rows + HALO) * par)], far),
        )
        halos.append(
            [
                remote(*ends[kind][:2], halo_send.at[kind, which], halo_recv.at[kind, which], ends[kind][2])
                for kind in range(3)
            ]
        )

    def columns(c):
        return pl.ds(pl.multiple_of(c * 128, 128), 128)

    def place(row):
        return pl.ds(pl.multiple_of(row, 32), rows)

    def send(c, kind, which):
        cols = columns(c)
        dst = kv.at[which]
        src = None if kind == 3 or not isinstance(which, int) else (k_hbm, v_hbm)[which]
        src = kv.at[which, pl.ds(2 * rows, rows)] if src is None else src
        src = src.at[:, cols]
        if kind == 0:
            args = src, dst.at[place(4 * rows * (1 - par)), cols], near
        elif kind == 1:
            args = src, dst.at[place(4 * rows * par), cols], far
        elif kind == 2:
            args = src, dst.at[place(rows + 2 * rows * par), cols], partner
        else:
            args = (
                dst.at[place(4 * rows * (1 - par)), cols],
                dst.at[place(3 * rows - 2 * rows * par), cols],
                partner,
            )
        return remote(
            args[0],
            args[1],
            send_sem.at[kind, c, which],
            recv_sem.at[kind, c, which],
            args[2],
        )

    def begin(kinds, which, first=0):
        def start_chunk(c, carry):
            for kind in kinds:
                send(c, kind, which).start()
            return carry

        lax.fori_loop(first, n_chunks, start_chunk, 0)

    for c in range(AHEAD):
        send(c, 0, 0).start()
        send(c, 1, 0).start()
    for kind in (1, 0):
        for pair in halos:
            pair[kind].start()
    begin((0,), 0, AHEAD)
    begin((2,), 0)
    for pair in halos:
        pair[1].wait_recv()
        pair[2].start()
    begin((1,), 0, AHEAD)
    begin((0, 2), 1)
    begin((1,), 1)

    for copy in small:
        copy.wait()
    lens_pad[...] = jnp.zeros(lens_pad.shape, jnp.float32)
    lens_pad[:, pl.ds(0, lens_ref.shape[1])] = lens_ref[...].astype(jnp.float32)
    lens = lens_pad[...]
    low = lax.broadcasted_iota(jnp.int32, (128, 128), 0)
    lane = lax.broadcasted_iota(jnp.int32, (128, 128), 1)
    wide = jnp.broadcast_to(lens, (128, 128))
    tall = jnp.sum(jnp.where(low == lane, wide, 0.0), axis=1, keepdims=True)
    ends = jnp.sum(jnp.where(low <= lane, tall, 0.0), axis=0, keepdims=True)
    starts = ends - lens

    def member(first, count):
        pos = first + lax.broadcasted_iota(jnp.int32, (count, 128), 0)
        pos = pos.astype(jnp.float32)
        return pos, (pos >= starts) & (pos < ends)

    base = me * rows
    for part in range(5):
        _, inside = member(base + (part - 2) * rows, rows)
        kf[pl.ds(part * rows, rows), :] = jnp.where(inside, 0.0, APART).astype(jnp.bfloat16)
    _, inside = member(base - HALO, q_rows)
    qf[...] = jnp.where(inside, 1.0, 0.0).astype(jnp.bfloat16)
    pos, inside = member(base, rows)
    first = jnp.sum(jnp.where(inside, starts, 0.0), axis=1, keepdims=True)
    final = jnp.sum(jnp.where(inside, ends, 0.0), axis=1, keepdims=True)
    shifted = rows + 8
    half = taps_ref.shape[0] // 2
    for room, value in ((before, pos - first), (after, final - 1.0 - pos)):
        room[pl.ds(0, 8), :] = jnp.full((8, 128), -1.0, jnp.float32)
        room[pl.ds(shifted, 8), :] = jnp.full((8, 128), -1.0, jnp.float32)
        room[pl.ds(8, rows), :] = jnp.broadcast_to(value, (rows, 128))
    for j in range(2 * half + 1):
        if j != half:
            room = before if j < half else after
            near_rows = room[pl.ds(8 - (j + 1) % 8, shifted), :]
            keeps[j] = jnp.where(near_rows >= float(abs(j - half)), 1.0, 0.0)

    for copy in own:
        copy.wait()
    for pair in halos:
        pair[0].wait_recv()
        pair[2].wait_recv()

    tile = q_rows // TILES
    window = WINDOW
    even = lax.broadcasted_iota(jnp.int32, (tile, 128), 1) < 64
    is_even = (lax.broadcasted_iota(jnp.int32, (1, 128), 1) < 64).astype(jnp.float32)
    lo = is_even.astype(jnp.bfloat16)
    hi = (1.0 - is_even).astype(jnp.bfloat16)
    ones = jnp.ones((window, 128), jnp.bfloat16)

    mxs[1] = jnp.zeros((q_rows, 128), jnp.float32)
    def weigh(c):
        cols = columns(c)
        for t in range(TILES):
            mine = pl.ds(t * tile, tile)
            keys = pl.ds(t * (span - window), window)
            qt = qb[mine, cols] * jnp.bfloat16(0.125)
            feat = qf[mine, :]
            q2 = jnp.concatenate(
                [
                    jnp.concatenate([qt * lo, feat], axis=1),
                    jnp.concatenate([qt * hi, feat], axis=1),
                ],
                axis=0,
            )
            kk = jnp.concatenate([kb[keys, cols], kf[keys, :]], axis=1)
            s = lax.dot_general(
                q2, kk, (((1,), (1,)), ((), ())), preferred_element_type=jnp.float32
            )
            m = jnp.max(s, axis=1, keepdims=True)
            pb[c * TILES + t] = jnp.exp(s - m).astype(jnp.bfloat16)

    def convolve(c, mx, cv):
        cols = columns(c)
        for y in range(0, shifted, CONV_ROWS):
            count = min(CONV_ROWS, shifted - y)
            for r in range(8):
                acc = None
                for j in range(taps_ref.shape[0]):
                    if (j + 1) % 8 == r:
                        x = mx[pl.ds(y + j + 1 - r, count), :]
                        if j != half:
                            x = x * keeps[j, pl.ds(y, count), :]
                        x = x * taps_ref[pl.ds(j, 1), cols]
                        acc = x if acc is None else acc + x
                lag[r, pl.ds(y, count), :] = acc
        for t in range(0, rows, CONV_ROWS):
            acc = lag[0, pl.ds(t, CONV_ROWS), :]
            for r in range(1, 8):
                acc = acc + lag[r, pl.ds(t + r, CONV_ROWS), :]
            cv[pl.ds(t, CONV_ROWS), cols] = acc

    def mix(c, mx):
        cols = columns(c)
        for t in range(TILES):
            mine = pl.ds(t * tile, tile)
            keys = pl.ds(t * (span - window), window)
            vv = jnp.concatenate([vb[keys, cols], ones], axis=1)
            o = jnp.dot(pb[c * TILES + t], vv, preferred_element_type=jnp.float32)
            num = jnp.where(even, o[:tile, :128], o[tile:, :128])
            den = jnp.where(even, o[:tile, 128:], o[tile:, 128:])
            mixed = rb[mine, cols].astype(jnp.float32) + num / den
            mx[mine, :] = mixed.astype(jnp.bfloat16).astype(jnp.float32)

    def take(i):
        which, c = i // n_chunks, i % n_chunks
        send(c, 0, which).wait_recv()
        send(c, 3, which).start()

    def ready(c, which):
        for kind in (2, 3, 1):
            send(c, kind, which).wait_recv()

    take(0)

    def weigh_step(c, carry):
        take(c + 1)
        ready(c, 0)
        weigh(c)
        return carry

    lax.fori_loop(0, n_chunks, weigh_step, 0)

    for pair in halos:
        for copy in pair:
            copy.wait_send()

    def keep(c, a):
        cols = columns(c)
        mb[:, cols] = mxs[a, pl.ds(HALO, rows), :].astype(jnp.bfloat16)

    def mix_step(j, carry):
        for a in (0, 1):
            c = 2 * j + a
            prev = lax.max(c - 1, 0)
            if a:
                convolve(prev, mxs.at[0], cv)
            else:

                @pl.when(c > 0)
                def _():
                    convolve(prev, mxs.at[1], cv)

            @pl.when(c + 1 < n_chunks)
            def _():
                take(n_chunks + c + 1)

            ready(c, 1)
            mix(c, mxs.at[a])
            keep(c, a)
            for kind in range(4):
                send(c, kind, 0).wait_send()

            @pl.when(c > 0)
            def _():
                for kind in range(4):
                    send(c - 1, kind, 1).wait_send()

        return carry

    lax.fori_loop(0, n_chunks // 2, mix_step, 0)
    convolve(n_chunks - 1, mxs.at[1], cv)

    for r in range(0, rows, NORM_ROWS):
        some = pl.ds(r, NORM_ROWS)
        x = cv[some, :]
        mean = jnp.sum(x, axis=1, keepdims=True) * (1.0 / width)
        x = x - mean
        var = jnp.sum(x * x, axis=1, keepdims=True) * (1.0 / width)
        normed = x * lax.rsqrt(var + 1e-05) * gain_ref[...] + shift_ref[...]
        gated = 0.5 * normed
        gated = gated + gated * jnp.tanh(gated)
        result = mb[some, :].astype(jnp.float32) + gated
        out_ref[some, :] = result.astype(out_ref.dtype)

    for kind in range(4):
        send(n_chunks - 1, kind, 1).wait_send()


def local(
    query_proj,
    key_proj,
    value_proj,
    residual_in,
    utter_lengths,
    depth_kernel,
    norm_gain,
    norm_shift,
):
    rows, width = query_proj.shape
    n = lax.axis_size("seq")
    n_chunks = width // 128
    q_rows, span = rows + 2 * HALO, 5 * rows
    vmem = pl.BlockSpec(memory_space=pltpu.VMEM)
    hbm = pl.BlockSpec(memory_space=pltpu.HBM)
    bf16, f32 = jnp.bfloat16, jnp.float32
    return pl.pallas_call(
        functools.partial(block_kernel, n),
        out_shape=jax.ShapeDtypeStruct((rows, width), bf16),
        in_specs=[hbm] * 8,
        out_specs=vmem,
        scratch_shapes=[
            pltpu.VMEM((1, utter_lengths.shape[0]), jnp.int32),
            pltpu.VMEM(depth_kernel.shape, f32),
            pltpu.VMEM((1, width), f32),
            pltpu.VMEM((1, width), f32),
            pltpu.VMEM((2, HALO, width), bf16),
            pltpu.VMEM((q_rows, width), bf16),
            pltpu.VMEM((q_rows, width), bf16),
            pltpu.VMEM((2, span, width), bf16),
            pltpu.VMEM((TILES * n_chunks, 2 * q_rows // TILES, WINDOW), bf16),
            pltpu.VMEM((1, 128), f32),
            pltpu.VMEM((span, 128), bf16),
            pltpu.VMEM((q_rows, 128), bf16),
            pltpu.VMEM((rows + 16, 128), f32),
            pltpu.VMEM((rows + 16, 128), f32),
            pltpu.VMEM((depth_kernel.shape[0], rows + 8, 128), f32),
            pltpu.VMEM((8, rows + 8, 128), f32),
            pltpu.VMEM((2, q_rows, 128), f32),
            pltpu.VMEM((rows, width), bf16),
            pltpu.VMEM((rows, width), f32),
            pltpu.SemaphoreType.DMA((4,)),
            pltpu.SemaphoreType.DMA((4,)),
            pltpu.SemaphoreType.DMA((3, 2)),
            pltpu.SemaphoreType.DMA((3, 2)),
            pltpu.SemaphoreType.DMA((4, n_chunks, 2)),
            pltpu.SemaphoreType.DMA((4, n_chunks, 2)),
        ],
        compiler_params=pltpu.CompilerParams(
            collective_id=0, has_side_effects=True, vmem_limit_bytes=44 << 20
        ),
        name="conformer_block",
    )(
        *(
            pltpu.with_memory_space_constraint(array, pltpu.HBM)
            for array in (
                utter_lengths.reshape(1, -1),
                depth_kernel,
                norm_gain.reshape(1, -1),
                norm_shift.reshape(1, -1),
                query_proj,
                key_proj,
                value_proj,
                residual_in,
            )
        )
    )


def solution(mesh):
    return jax.shard_map(
        local,
        mesh=mesh,
        in_specs=(
            P(("dp", "seq"), None),
            P(("dp", "seq"), None),
            P(("dp", "seq"), None),
            P(("dp", "seq"), None),
            P("dp"),
            P(),
            P(),
            P(),
        ),
        out_specs=P(("dp", "seq"), None),
        check_vma=False,
    )
```
